32 devices in a mesh: groups: 2 (over x), dp: 8 (over z, y), split: 2 (over core).
Axes of the slice: x: 2, y: 2, z: 4, core: 2. Of those that a mesh axis runs over, the one named last changes fastest.
Arguments:
- embeddings: bfloat16 [65536, 512], P(('groups', 'dp', 'split')), parts along dimension 0, may hold values from -6 to 6
- assignment: int32 [65536, 1], P(('groups', 'dp', 'split')), parts along dimension 0, may hold values from 0 to 15; in each aligned block of 2048 rows (0 to 2047, 2048 to 4095, ...) at most 192 rows name the same one
- order_key: int32 [65536], P(('groups', 'dp', 'split')), parts along dimension 0, may hold values from 0 to 32767, each once
Outputs:
- nearest: float32 [65536], P(('groups', 'dp', 'split')), parts along dimension 0
The draws below stay inside these ranges and needn't reach their ends.
There are 2 independent parts, one for each index of `groups`. The reference program is written for one: setup_inputs(seed, part) draws one part's arguments, and reference() takes and returns one part's arrays. A program takes and returns all parts, laid end to end along the dimension named above; each array names one. Nothing has to cross between parts.
Inputs may be any that keep to these rules, and one draw needn't show every extreme that they name: `assignment`: in each device's 2048 rows no cluster has more than 192 rows, and some cluster has exactly 192. `order_key`: all values within a part are distinct.
All inputs are finite; a program needn't handle non-finite values.
Results may differ from the reference program's by a relative error of at most 0.0013.
Values may be sent and summed in bfloat16 or wider, within the bound.
A program may use at most 64 MiB of HBM per device.

```python
import math
import jax
import jax.numpy as jnp
import numpy as np
from jax import lax

D = 512
ROWS_DEV = 2048
CLUSTERS = 16
MOST = 192
ROWS = 32768
N_DP = 8
N_SPLIT = 2


def levels(key, extent, pieces, least, top_value):
    def one(dim, blocks):
        steps = jax.random.uniform(jax.random.fold_in(jax.random.fold_in(key, 6), dim), (blocks,), jnp.float32, least / len(pieces), top_value / len(pieces))
        return jnp.repeat(jnp.exp(steps), extent[dim] // blocks).reshape((-1,) + (1,) * (len(extent) - dim - 1))

    loudness = one(*pieces[0])
    for cut in pieces[1:]:
        loudness = loudness * one(*cut)
    return loudness


def routed_block(key, own, number, rows, count, top, reach, lean):
    order = jax.random.permutation(key, count)
    crowded, usual = load_shares(count, rows * top, reach, lean, True), load_shares(count, rows * top, reach, lean, False)
    places = jnp.arange(count)

    def named(tallies, rotation):
        used = int((tallies > 0).sum())
        fixed = max(1, used // 4)
        shifted = fixed + (places - fixed + rotation * (used - fixed)) % max(1, count - fixed)
        return jnp.zeros((count,), jnp.int32).at[order[jnp.where(places < fixed, places, shifted)]].set(jnp.asarray(tallies, jnp.int32))

    tallies = jnp.where(number % 4 == 0, named(crowded, number // 4), named(usual, number - number // 4 - 1))
    mixed = jax.random.permutation(jax.random.fold_in(own, 3), count)
    donor, receiver = mixed[0:count // 2 * 2:2], mixed[1:count // 2 * 2:2]
    slack = jnp.minimum(tallies[donor] - 1, reach - tallies[receiver]) // 2
    slack = jnp.where((donor == order[0]) | (receiver == order[0]) | (tallies[receiver] == 0), 0, jnp.maximum(slack, 0))
    shifted = jax.random.randint(jax.random.fold_in(own, 4), (count // 2,), 0, 1 << 20) % (slack + 1)
    tallies = tallies.at[donor].add(-shifted).at[receiver].add(shifted)
    labels = jnp.searchsorted(jnp.cumsum(tallies), jnp.arange(rows * top), side="right").astype(jnp.int32)
    table = labels.reshape(top, rows).T
    table = table[jax.random.permutation(jax.random.fold_in(own, 1), rows)]
    rotation = jax.random.randint(jax.random.fold_in(own, 2), (rows, 1), 0, top)
    return jnp.take_along_axis(table, (jnp.arange(top)[None, :] + rotation) % top, axis=1)


def load_shares(amount, total, limit, lean, full):
    portions = [(1 << 20) // math.isqrt(standing ** lean) + 1 for standing in range(1, amount + 1)]
    largest = limit if full else min(limit, max(-(-total // amount), total * portions[0] // sum(portions)))
    least = 1 if total - largest >= amount - 1 else 0
    given, spare = [largest] + [least] * (amount - 1), total - largest - least * (amount - 1)
    while spare > 0:
        free = [i for i in range(1, amount) if given[i] < largest] or [i for i in range(1, amount) if given[i] < limit]
        mass, remaining = sum([portions[i] for i in free]), spare
        for i in free:
            addition = min(limit - given[i], max(1, remaining * portions[i] // mass), spare)
            given[i] = given[i] + addition
            spare = spare - addition
    return np.array(given)


def noise(key, shape, scale, bound, pieces=(), kind=jnp.bfloat16):
    level = levels(key, shape, pieces, -0.22, 0.18) if pieces else 1.0
    entries = jax.random.normal(key, shape, jnp.float32) * scale * level
    return jnp.minimum(jnp.maximum(entries, -bound), bound).astype(kind)


def setup_inputs(seed: int = 0, part: int = 0) -> dict:
    streams_of = jax.random.split(jax.random.key(seed), 4)
    own_keys = jax.random.split(jax.random.fold_in(streams_of[3], part), 4)
    embeddings = noise(own_keys[0], (ROWS, D), 1.0, 6.0, ((0, 16),))
    assignment_keys = jax.random.split(jax.random.fold_in(own_keys[1], 1), ROWS // ROWS_DEV)
    assignment_turns = jax.random.permutation(jax.random.fold_in(own_keys[1], 3), ROWS // ROWS_DEV)
    assignment = jax.vmap(lambda own, number: routed_block(jax.random.fold_in(own_keys[1], 2), own, number, ROWS_DEV, CLUSTERS, 1, MOST, 2))(assignment_keys, assignment_turns).reshape((ROWS, 1))
    order_key = jax.random.permutation(own_keys[2], ROWS).astype(jnp.int32)
    return {"embeddings": embeddings, "assignment": assignment, "order_key": order_key}


def reference(embeddings, assignment, order_key):
    values = embeddings.astype(jnp.float32)
    scale = lax.rsqrt(lax.optimization_barrier(jnp.sum(values * values, axis=1, keepdims=True)) + 1e-06)
    unit = (values * scale).astype(jnp.bfloat16).astype(jnp.float32)
    cluster = assignment[:, 0].astype(jnp.int32)
    capacity = N_SPLIT * N_DP * MOST
    ordering = jnp.argsort(cluster, stable=True).astype(jnp.int32)
    sorted_cluster = cluster[ordering]
    onehot = (cluster[:, None] == jnp.arange(CLUSTERS, dtype=jnp.int32)[None, :]).astype(jnp.int32)
    counts = lax.optimization_barrier(jnp.sum(onehot, axis=0))
    starts = (jnp.cumsum(counts) - counts).astype(jnp.int32)
    padded_unit = jnp.concatenate([unit[ordering], jnp.zeros((capacity, D), unit.dtype)], axis=0)
    padded_key = jnp.concatenate([order_key[ordering].astype(jnp.int32), jnp.zeros((capacity,), jnp.int32)], axis=0)
    padded_cluster = jnp.concatenate([sorted_cluster, jnp.full((capacity,), -1, jnp.int32)], axis=0)

    def one_cluster(index):
        begin = starts[index]
        block = lax.dynamic_slice(padded_unit, (begin, jnp.int32(0)), (capacity, D))
        keys = lax.dynamic_slice(padded_key, (begin,), (capacity,))
        members = lax.dynamic_slice(padded_cluster, (begin,), (capacity,))
        sims = jnp.dot(block, block.T, precision=lax.Precision.HIGHEST)
        allowed = (members[None, :] == index) & (keys[None, :] < keys[:, None])
        return lax.optimization_barrier(jnp.max(jnp.where(allowed, sims, -1.0), axis=1))
    table = lax.map(one_cluster, jnp.arange(CLUSTERS, dtype=jnp.int32))
    position = jnp.arange(ROWS, dtype=jnp.int32) - starts[sorted_cluster]
    result_sorted = table[sorted_cluster, position]
    nearest = jnp.zeros((ROWS,), result_sorted.dtype).at[ordering].set(result_sorted)
    return nearest
```

```python
import functools

import jax
import jax.numpy as jnp
from jax import lax
from jax.experimental import pallas as pl
from jax.experimental.pallas import tpu as pltpu
from jax.sharding import PartitionSpec as P

epsilon = 1e-06
MESH = pl.DeviceIdType.MESH
NT = (((1,), (1,)), ((), ()))
BLOCK = 256
SUB = 8


def xor(a, b, n):
    total, bit = 0, 1
    while bit < n:
        p, q = (a // bit) % 2, (b // bit) % 2
        total = total + (p + q - 2 * p * q) * bit
        bit *= 2
    return total


def offset_of(slot, n):
    t = slot - 1
    near = t % 2
    return (1 - near) * (n // 2 + t // 2) + near * ((t + 1) // 2 % (n // 2))


def kernel(n, n_split, most, rows_ref, cluster_ref, key_ref, out_ref,
           slot_ref, send, send_key, recv, recv_key, lane_key, sub_key, best, back_send, back,
           row_ssem, row_rsem, key_ssem, key_rsem, back_ssem, back_rsem):
    f32, bf16, i32 = jnp.float32, jnp.bfloat16, jnp.int32
    rows = rows_ref.shape[0]
    me = lax.axis_index("dp") * n_split + lax.axis_index("split")

    def device(slot):
        partner = xor(me, offset_of(slot, n), n)
        return {"dp": partner // n_split, "split": partner % n_split}

    barrier = pltpu.get_barrier_semaphore()

    @pl.loop(1, n)
    def _(slot):
        pl.semaphore_signal(barrier, inc=1, device_id=device(slot), device_id_type=MESH)

    before = (lax.broadcasted_iota(i32, (BLOCK, BLOCK), 0) < lax.broadcasted_iota(i32, (BLOCK, BLOCK), 1))
    before = jnp.where(before, 1.0, 0.0).astype(bf16)
    carry = jnp.zeros((n, 1), f32)
    for start in range(0, rows, BLOCK):
        here = cluster_ref[:, start:start + BLOCK]
        onehot = jnp.where(lax.broadcasted_iota(i32, (n, BLOCK), 0) == here, 1.0, 0.0)
        earlier = jnp.dot(onehot.astype(bf16), before, preferred_element_type=f32) + carry
        carry = carry + jnp.sum(onehot, axis=1, keepdims=True)
        rank = jnp.sum(onehot * earlier, axis=0, keepdims=True).astype(i32)
        slot_ref[:, start:start + BLOCK] = here * most + rank

    key = key_ref[...]
    digit = lax.broadcasted_iota(i32, (SUB, rows), 0)
    digits = jnp.where(digit == 0, key // 16384, jnp.where(digit == 1, (key // 128) % 128, jnp.where(digit == 2, key % 128, jnp.where(digit == 3, 1, 0))))
    digits = digits.astype(f32).astype(bf16)

    def weights(shape, dim):
        place = lax.broadcasted_iota(i32, shape, dim)
        w = jnp.where(place == 0, 16384.0, jnp.where(place == 1, 128.0, jnp.where(place == 2, 1.0, jnp.where(place == 3, -4194304.0, 0.0))))
        return w.astype(bf16)

    same = lax.broadcasted_iota(i32, (most, most), 0) == lax.broadcasted_iota(i32, (most, most), 1)
    identity = jnp.where(same, 1.0, 0.0).astype(bf16)

    def pack(cluster):
        place = slot_ref[...] - cluster * most
        pick = jnp.where(lax.broadcasted_iota(i32, (most, rows), 0) == place, 1.0, 0.0).astype(bf16)
        values = jnp.dot(pick, rows_ref[...], preferred_element_type=f32)
        scale = lax.rsqrt(jnp.sum(values * values, axis=1, keepdims=True) + epsilon)
        return (values * scale).astype(bf16), lax.dot_general(digits, pick, NT, preferred_element_type=f32)

    def row_copy(slot):
        return pltpu.make_async_remote_copy(send.at[slot], recv.at[slot], row_ssem.at[slot], row_rsem.at[slot], device_id=device(slot), device_id_type=MESH)

    def key_copy(slot):
        return pltpu.make_async_remote_copy(send_key.at[slot], recv_key.at[slot], key_ssem.at[slot], key_rsem.at[slot], device_id=device(slot), device_id_type=MESH)

    def back_copy(slot, cluster):
        return pltpu.make_async_remote_copy(back_send.at[slot], back.at[cluster], back_ssem.at[slot], back_rsem.at[slot], device_id=device(slot), device_id_type=MESH)

    send[1], send_key[1] = pack(xor(me, offset_of(1, n), n))
    pl.semaphore_wait(barrier, n - 1)

    @pl.loop(2, n + 1)
    def _(slot):
        row_copy(slot - 1).start()
        key_copy(slot - 1).start()
        at = slot % n
        packed, packed_key = pack(xor(me, offset_of(slot, n), n))
        send[at] = packed
        send_key[at] = packed_key

    def take(slot, new, digits_in):
        parts = digits_in.astype(bf16)
        lane_key[slot] = jnp.dot(weights((SUB, SUB), 1), parts, preferred_element_type=f32)
        turned = lax.dot_general(identity, parts, NT, preferred_element_type=f32).astype(bf16)
        sub_key[slot] = jnp.dot(turned, weights((SUB, 128), 0), preferred_element_type=f32)

    def tile(columns, columns_key, own, own_key):
        sims = lax.dot_general(columns, own, NT, preferred_element_type=f32)
        seen = jnp.where(columns_key < own_key, sims, -1.0)
        return jnp.max(seen.reshape(most // SUB, SUB, most), axis=0)

    recv[0] = send[0]
    take(0, send[0], send_key[0])
    best[0] = jnp.maximum(tile(recv[0], sub_key[0][:, :1], recv[0], lane_key[0][:1]), -1.0)

    @pl.loop(1, n)
    def _(u):
        row_copy(u).wait_recv()
        key_copy(u).wait_recv()
        new = recv[u]
        take(u, new, recv_key[u])
        new_lane, new_sub = lane_key[u][:1], sub_key[u][:, :1]

        def meet(i, running):
            other = recv[i]
            best[i] = jnp.maximum(best[i], tile(new, new_sub, other, lane_key[i][:1]))
            return jnp.maximum(running, tile(other, sub_key[i][:, :1], new, new_lane))

        best[u] = lax.fori_loop(0, u, meet, tile(new, new_sub, new, new_lane))

    part = lax.broadcasted_iota(i32, (SUB, most), 0)

    def parts_of(slot):
        whole = jnp.broadcast_to(jnp.max(best[slot], axis=0, keepdims=True), (SUB, most))
        high = whole.astype(bf16).astype(f32)
        middle = (whole - high).astype(bf16).astype(f32)
        low = (whole - high) - middle
        return jnp.where(part == 0, high, jnp.where(part == 1, middle, jnp.where(part == 2, low, 0.0)))

    @pl.loop(1, n)
    def _(slot):
        back_send[slot] = parts_of(slot)

    back[me] = parts_of(0)

    @pl.loop(1, n)
    def _(slot):
        back_copy(slot, me).start()

    @pl.loop(1, n)
    def _(slot):
        row_copy(slot).wait_send()
        key_copy(slot).wait_send()

    @pl.loop(1, n)
    def _(slot):
        back_copy(slot, xor(me, offset_of(slot, n), n)).wait_recv()

    turned = lax.dot_general(identity, back[...].reshape(n * SUB, most).astype(bf16), NT, preferred_element_type=f32).astype(bf16)
    for start in range(0, rows, BLOCK):
        here = cluster_ref[:, start:start + BLOCK]
        rank = slot_ref[:, start:start + BLOCK] - here * most
        onehot = jnp.where(lax.broadcasted_iota(i32, (n * SUB, BLOCK), 0) // SUB == here, 1.0, 0.0).astype(bf16)
        found = jnp.dot(turned, onehot, preferred_element_type=f32)
        found = jnp.where(lax.broadcasted_iota(i32, (most, BLOCK), 0) == rank, found, 0.0)
        out_ref[:, start:start + BLOCK] = jnp.sum(found, axis=0, keepdims=True)

    @pl.loop(1, n)
    def _(slot):
        back_copy(slot, me).wait_send()


def per_device(embeddings, assignment, order_key):
    rows, width = embeddings.shape
    n_split = lax.axis_size("split")
    n = lax.axis_size("dp") * n_split
    most = 3 * rows // (2 * n)
    f32, bf16 = jnp.float32, jnp.bfloat16
    vmem = pl.BlockSpec(memory_space=pltpu.VMEM)
    dma = pltpu.SemaphoreType.DMA((n,))
    nearest = pl.pallas_call(
        functools.partial(kernel, n, n_split, most),
        out_shape=jax.ShapeDtypeStruct((1, rows), f32),
        in_specs=[vmem] * 3,
        out_specs=vmem,
        scratch_shapes=[
            pltpu.VMEM((1, rows), jnp.int32),
            pltpu.VMEM((n, most, width), bf16),
            pltpu.VMEM((n, SUB, most), f32),
            pltpu.VMEM((n, most, width), bf16),
            pltpu.VMEM((n, SUB, most), f32),
            pltpu.VMEM((n, SUB, most), f32),
            pltpu.VMEM((n, most, 128), f32),
            pltpu.VMEM((n, SUB, most), f32),
            pltpu.VMEM((n, SUB, most), f32),
            pltpu.VMEM((n, SUB, most), f32),
            dma, dma, dma, dma, dma, dma,
        ],
        compiler_params=pltpu.CompilerParams(collective_id=0, has_side_effects=True, vmem_limit_bytes=56 * 1024 * 1024),
    )(embeddings, assignment.reshape(1, rows), order_key.reshape(1, rows))
    return nearest.reshape(rows)


def solution(mesh):
    placed = (
        P(("groups", "dp", "split"), None),
        P(("groups", "dp", "split"), None),
        P(("groups", "dp", "split")),
    )
    return jax.shard_map(
        per_device,
        mesh=mesh,
        in_specs=placed,
        out_specs=P(("groups", "dp", "split")),
        check_vma=False,
    )
```

```python
import functools

import jax
import jax.numpy as jnp
from jax import lax
from jax.experimental import pallas as pl
from jax.experimental.pallas import tpu as pltpu
from jax.sharding import PartitionSpec as P

epsilon = 1e-06
MESH = pl.DeviceIdType.MESH
NT = (((1,), (1,)), ((), ()))
BLOCK = 256
SUB = 8
GROUP = 4


def xor(a, b, n):
    total, bit = 0, 1
    while bit < n:
        p, q = (a // bit) % 2, (b // bit) % 2
        total = total + (p + q - 2 * p * q) * bit
        bit *= 2
    return total


def offset_of(slot, n):
    t = slot - 1
    near = t % 2
    return (1 - near) * (n // 2 + t // 2) + near * ((t + 1) // 2 % (n // 2))


def kernel(n, n_split, most, rows_ref, cluster_ref, key_ref, out_ref,
           slot_ref, send, send_key, recv, recv_key, lane_key, sub_key, best, back_send, back,
           row_ssem, row_rsem, key_ssem, key_rsem, back_ssem, back_rsem):
    f32, bf16, i32 = jnp.float32, jnp.bfloat16, jnp.int32
    rows = rows_ref.shape[0]
    me = lax.axis_index("dp") * n_split + lax.axis_index("split")

    def device(slot):
        partner = xor(me, offset_of(slot, n), n)
        return {"dp": partner // n_split, "split": partner % n_split}

    barrier = pltpu.get_barrier_semaphore()

    @pl.loop(1, n)
    def _(slot):
        pl.semaphore_signal(barrier, inc=1, device_id=device(slot), device_id_type=MESH)

    before = (lax.broadcasted_iota(i32, (BLOCK, BLOCK), 0) < lax.broadcasted_iota(i32, (BLOCK, BLOCK), 1))
    before = jnp.where(before, 1.0, 0.0).astype(bf16)
    carry = jnp.zeros((n, 1), f32)
    for start in range(0, rows, BLOCK):
        here = cluster_ref[:, start:start + BLOCK]
        onehot = jnp.where(lax.broadcasted_iota(i32, (n, BLOCK), 0) == here, 1.0, 0.0)
        earlier = jnp.dot(onehot.astype(bf16), before, preferred_element_type=f32) + carry
        carry = carry + jnp.sum(onehot, axis=1, keepdims=True)
        rank = jnp.sum(onehot * earlier, axis=0, keepdims=True).astype(i32)
        slot_ref[:, start:start + BLOCK] = here * most + rank

    key = key_ref[...]
    digit = lax.broadcasted_iota(i32, (SUB, rows), 0)
    digits = jnp.where(digit == 0, key // 16384, jnp.where(digit == 1, (key // 128) % 128, jnp.where(digit == 2, key % 128, jnp.where(digit == 3, 1, 0))))
    digits = digits.astype(f32).astype(bf16)

    def weights(shape, dim):
        place = lax.broadcasted_iota(i32, shape, dim)
        w = jnp.where(place == 0, 16384.0, jnp.where(place == 1, 128.0, jnp.where(place == 2, 1.0, jnp.where(place == 3, -4194304.0, 0.0))))
        return w.astype(bf16)

    same = lax.broadcasted_iota(i32, (most, most), 0) == lax.broadcasted_iota(i32, (most, most), 1)
    identity = jnp.where(same, 1.0, 0.0).astype(bf16)

    def pack(cluster):
        place = slot_ref[...] - cluster * most
        pick = jnp.where(lax.broadcasted_iota(i32, (most, rows), 0) == place, 1.0, 0.0).astype(bf16)
        values = jnp.dot(pick, rows_ref[...], preferred_element_type=f32)
        scale = lax.rsqrt(jnp.sum(values * values, axis=1, keepdims=True) + epsilon)
        return (values * scale).astype(bf16), lax.dot_general(digits, pick, NT, preferred_element_type=f32)

    def row_copy(slot):
        return pltpu.make_async_remote_copy(send.at[slot], recv.at[slot], row_ssem.at[slot], row_rsem.at[slot], device_id=device(slot), device_id_type=MESH)

    def key_copy(slot):
        return pltpu.make_async_remote_copy(send_key.at[slot], recv_key.at[slot], key_ssem.at[slot], key_rsem.at[slot], device_id=device(slot), device_id_type=MESH)

    def back_copy(slot, cluster):
        return pltpu.make_async_remote_copy(back_send.at[slot], back.at[cluster], back_ssem.at[slot], back_rsem.at[slot], device_id=device(slot), device_id_type=MESH)

    send[1], send_key[1] = pack(xor(me, offset_of(1, n), n))
    pl.semaphore_wait(barrier, n - 1)

    @pl.loop(2, n + 1)
    def _(slot):
        row_copy(slot - 1).start()
        key_copy(slot - 1).start()
        at = slot % n
        packed, packed_key = pack(xor(me, offset_of(slot, n), n))
        send[at] = packed
        send_key[at] = packed_key

    def take(slot, new, digits_in):
        parts = digits_in.astype(bf16)
        lane_key[slot] = jnp.dot(weights((SUB, SUB), 1), parts, preferred_element_type=f32)
        turned = lax.dot_general(identity, parts, NT, preferred_element_type=f32).astype(bf16)
        sub_key[slot] = jnp.dot(turned, weights((SUB, most), 0), preferred_element_type=f32)

    def tile(columns, columns_key, own, own_key):
        sims = lax.dot_general(columns, own, NT, preferred_element_type=f32)
        seen = jnp.where(columns_key < own_key, sims, -1.0)
        return jnp.max(seen.reshape(most // SUB, SUB, most), axis=0)

    recv[0] = send[0]
    take(0, send[0], send_key[0])
    best[0] = jnp.maximum(tile(recv[0], sub_key[0], recv[0], lane_key[0][:1]), -1.0)

    @pl.loop(1, n)
    def _(u):
        row_copy(u).wait_recv()
        key_copy(u).wait_recv()
        new = recv[u]
        take(u, new, recv_key[u])
        new_lane, new_sub = lane_key[u][:1], sub_key[u]

        def meet(i, running):
            other = recv[i]
            best[i] = jnp.maximum(best[i], tile(new, new_sub, other, lane_key[i][:1]))
            return jnp.maximum(running, tile(other, sub_key[i], new, new_lane))

        def meet_group(group, running):
            for i in range(GROUP):
                running = meet(group * GROUP + i, running)
            return running

        running = lax.fori_loop(0, u // GROUP, meet_group, tile(new, new_sub, new, new_lane))
        best[u] = lax.fori_loop(u // GROUP * GROUP, u, meet, running)

    part = lax.broadcasted_iota(i32, (SUB, most), 0)

    def parts_of(slot):
        whole = jnp.broadcast_to(jnp.max(best[slot], axis=0, keepdims=True), (SUB, most))
        high = whole.astype(bf16).astype(f32)
        middle = (whole - high).astype(bf16).astype(f32)
        low = (whole - high) - middle
        return jnp.where(part == 0, high, jnp.where(part == 1, middle, jnp.where(part == 2, low, 0.0)))

    @pl.loop(1, n)
    def _(slot):
        back_send[slot] = parts_of(slot)

    back[me] = parts_of(0)

    @pl.loop(1, n)
    def _(slot):
        back_copy(slot, me).start()

    @pl.loop(1, n)
    def _(slot):
        row_copy(slot).wait_send()
        key_copy(slot).wait_send()

    @pl.loop(1, n)
    def _(slot):
        back_copy(slot, xor(me, offset_of(slot, n), n)).wait_recv()

    turned = lax.dot_general(identity, back[...].reshape(n * SUB, most).astype(bf16), NT, preferred_element_type=f32).astype(bf16)
    for start in range(0, rows, BLOCK):
        here = cluster_ref[:, start:start + BLOCK]
        rank = slot_ref[:, start:start + BLOCK] - here * most
        onehot = jnp.where(lax.broadcasted_iota(i32, (n * SUB, BLOCK), 0) // SUB == here, 1.0, 0.0).astype(bf16)
        found = jnp.dot(turned, onehot, preferred_element_type=f32)
        found = jnp.where(lax.broadcasted_iota(i32, (most, BLOCK), 0) == rank, found, 0.0)
        out_ref[:, start:start + BLOCK] = jnp.sum(found, axis=0, keepdims=True)

    @pl.loop(1, n)
    def _(slot):
        back_copy(slot, me).wait_send()


def per_device(embeddings, assignment, order_key):
    rows, width = embeddings.shape
    n_split = lax.axis_size("split")
    n = lax.axis_size("dp") * n_split
    most = 3 * rows // (2 * n)
    f32, bf16 = jnp.float32, jnp.bfloat16
    vmem = pl.BlockSpec(memory_space=pltpu.VMEM)
    dma = pltpu.SemaphoreType.DMA((n,))
    nearest = pl.pallas_call(
        functools.partial(kernel, n, n_split, most),
        out_shape=jax.ShapeDtypeStruct((1, rows), f32),
        in_specs=[vmem] * 3,
        out_specs=vmem,
        scratch_shapes=[
            pltpu.VMEM((1, rows), jnp.int32),
            pltpu.VMEM((n, most, width), bf16),
            pltpu.VMEM((n, SUB, most), f32),
            pltpu.VMEM((n, most, width), bf16),
            pltpu.VMEM((n, SUB, most), f32),
            pltpu.VMEM((n, SUB, most), f32),
            pltpu.VMEM((n, most, most), f32),
            pltpu.VMEM((n, SUB, most), f32),
            pltpu.VMEM((n, SUB, most), f32),
            pltpu.VMEM((n, SUB, most), f32),
            dma, dma, dma, dma, dma, dma,
        ],
        compiler_params=pltpu.CompilerParams(collective_id=0, has_side_effects=True, vmem_limit_bytes=56 * 1024 * 1024),
    )(embeddings, assignment.reshape(1, rows), order_key.reshape(1, rows))
    return nearest.reshape(rows)


def solution(mesh):
    placed = (
        P(("groups", "dp", "split"), None),
        P(("groups", "dp", "split"), None),
        P(("groups", "dp", "split")),
    )
    return jax.shard_map(
        per_device,
        mesh=mesh,
        in_specs=placed,
        out_specs=P(("groups", "dp", "split")),
        check_vma=False,
    )
```

```python
import functools

import jax
import jax.numpy as jnp
from jax import lax
from jax.experimental import pallas as pl
from jax.experimental.pallas import tpu as pltpu
from jax.sharding import PartitionSpec as P

epsilon = 1e-06
MESH = pl.DeviceIdType.MESH
NT = (((1,), (1,)), ((), ()))
BLOCK = 256
SUB = 8
GROUP = 4


def xor(a, b, n):
    total, bit = 0, 1
    while bit < n:
        p, q = (a // bit) % 2, (b // bit) % 2
        total = total + (p + q - 2 * p * q) * bit
        bit *= 2
    return total


def offset_of(slot, n):
    t = slot - 1
    near = t % 2
    return (1 - near) * (n // 2 + t // 2) + near * ((t + 1) // 2 % (n // 2))


def kernel(n, n_split, most, rows_hbm, cluster_ref, key_ref, out_ref,
           rows_ref, rows_sem, slot_ref, send, send_key, recv, recv_key, lane_key, sub_key, best, back_send, back, back_parts,
           row_ssem, row_rsem, key_ssem, key_rsem, back_ssem, back_rsem):
    f32, bf16, i32 = jnp.float32, jnp.bfloat16, jnp.int32
    rows = rows_ref.shape[0]
    fetch = pltpu.make_async_copy(rows_hbm, rows_ref, rows_sem)
    fetch.start()
    me = lax.axis_index("dp") * n_split + lax.axis_index("split")

    def device(slot):
        partner = xor(me, offset_of(slot, n), n)
        return {"dp": partner // n_split, "split": partner % n_split}

    barrier = pltpu.get_barrier_semaphore()

    @pl.loop(1, n)
    def _(slot):
        pl.semaphore_signal(barrier, inc=1, device_id=device(slot), device_id_type=MESH)

    before = (lax.broadcasted_iota(i32, (BLOCK, BLOCK), 0) < lax.broadcasted_iota(i32, (BLOCK, BLOCK), 1))
    before = jnp.where(before, 1.0, 0.0).astype(bf16)
    carry = jnp.zeros((n, 1), f32)
    for start in range(0, rows, BLOCK):
        here = cluster_ref[:, start:start + BLOCK]
        onehot = jnp.where(lax.broadcasted_iota(i32, (n, BLOCK), 0) == here, 1.0, 0.0)
        earlier = jnp.dot(onehot.astype(bf16), before, preferred_element_type=f32) + carry
        carry = carry + jnp.sum(onehot, axis=1, keepdims=True)
        rank = jnp.sum(onehot * earlier, axis=0, keepdims=True).astype(i32)
        slot_ref[:, start:start + BLOCK] = here * most + rank

    key = key_ref[...]
    digit = lax.broadcasted_iota(i32, (SUB, rows), 0)
    digits = jnp.where(digit == 0, key // 16384, jnp.where(digit == 1, (key // 128) % 128, jnp.where(digit == 2, key % 128, jnp.where(digit == 3, 1, 0))))
    digits = digits.astype(f32).astype(bf16)

    place = lax.broadcasted_iota(i32, (SUB, SUB), 1)
    combine = jnp.where(place == 0, 16384.0, jnp.where(place == 1, 128.0, jnp.where(place == 2, 1.0, jnp.where(place == 3, -4194304.0, 0.0)))).astype(bf16)
    part = lax.broadcasted_iota(i32, (SUB, most), 0)

    def parts_of(row):
        whole = jnp.broadcast_to(row, (SUB, most))
        high = whole.astype(bf16).astype(f32)
        middle = (whole - high).astype(bf16).astype(f32)
        low = (whole - high) - middle
        return jnp.where(part == 0, high, jnp.where(part == 1, middle, jnp.where(part == 2, low, 0.0)))

    same = lax.broadcasted_iota(i32, (most, most), 0) == lax.broadcasted_iota(i32, (most, most), 1)
    identity = jnp.where(same, 1.0, 0.0).astype(bf16)

    def pack(cluster):
        place = slot_ref[...] - cluster * most
        pick = jnp.where(lax.broadcasted_iota(i32, (most, rows), 0) == place, 1.0, 0.0).astype(bf16)
        values = jnp.dot(pick, rows_ref[...], preferred_element_type=f32)
        scale = lax.rsqrt(jnp.sum(values * values, axis=1, keepdims=True) + epsilon)
        picked = lax.dot_general(digits, pick, NT, preferred_element_type=f32)
        return (values * scale).astype(bf16), jnp.dot(combine, picked.astype(bf16), preferred_element_type=f32)[:1]

    def row_copy(slot):
        return pltpu.make_async_remote_copy(send.at[slot], recv.at[slot], row_ssem.at[slot], row_rsem.at[slot], device_id=device(slot), device_id_type=MESH)

    def key_copy(slot):
        return pltpu.make_async_remote_copy(send_key.at[slot], recv_key.at[slot], key_ssem.at[slot], key_rsem.at[slot], device_id=device(slot), device_id_type=MESH)

    def back_copy(slot, cluster):
        return pltpu.make_async_remote_copy(back_send.at[slot], back.at[cluster], back_ssem.at[slot], back_rsem.at[slot], device_id=device(slot), device_id_type=MESH)

    fetch.wait()
    send[1], send_key[1] = pack(xor(me, offset_of(1, n), n))
    pl.semaphore_wait(barrier, n - 1)

    @pl.loop(2, n + 1)
    def _(slot):
        row_copy(slot - 1).start()
        key_copy(slot - 1).start()
        at = slot % n
        packed, packed_key = pack(xor(me, offset_of(slot, n), n))
        send[at] = packed
        send_key[at] = packed_key

    def take(slot, row):
        lane_key[slot] = jnp.broadcast_to(row, (SUB, most))
        turned = lax.dot_general(identity, parts_of(row).astype(bf16), NT, preferred_element_type=f32).astype(bf16)
        sub_key[slot] = jnp.dot(turned, jnp.ones((SUB, most), bf16), preferred_element_type=f32)

    def tile(columns, columns_key, own, own_key):
        sims = lax.dot_general(columns, own, NT, preferred_element_type=f32)
        seen = jnp.where(columns_key < own_key, sims, -1.0)
        return jnp.max(seen.reshape(most // SUB, SUB, most), axis=0)

    recv[0] = send[0]
    take(0, send_key[0])
    best[0] = jnp.maximum(tile(recv[0], sub_key[0], recv[0], lane_key[0][:1]), -1.0)

    @pl.loop(1, n)
    def _(u):
        row_copy(u).wait_recv()
        key_copy(u).wait_recv()
        new = recv[u]
        take(u, recv_key[u])
        new_lane, new_sub = lane_key[u][:1], sub_key[u]

        def meet(i, running):
            other = recv[i]
            best[i] = jnp.maximum(best[i], tile(new, new_sub, other, lane_key[i][:1]))
            return jnp.maximum(running, tile(other, sub_key[i], new, new_lane))

        def meet_group(group, running):
            for i in range(GROUP):
                running = meet(group * GROUP + i, running)
            return running

        running = lax.fori_loop(0, u // GROUP, meet_group, tile(new, new_sub, new, new_lane))
        best[u] = lax.fori_loop(u // GROUP * GROUP, u, meet, running)

    @pl.loop(1, n)
    def _(slot):
        back_send[slot] = jnp.max(best[slot], axis=0, keepdims=True)

    back_parts[me] = parts_of(jnp.max(best[0], axis=0, keepdims=True))

    @pl.loop(1, n)
    def _(slot):
        back_copy(slot, me).start()

    @pl.loop(1, n)
    def _(slot):
        row_copy(slot).wait_send()
        key_copy(slot).wait_send()

    @pl.loop(1, n)
    def _(slot):
        cluster = xor(me, offset_of(slot, n), n)
        back_copy(slot, cluster).wait_recv()
        back_parts[cluster] = parts_of(back[cluster])

    turned = lax.dot_general(identity, back_parts[...].reshape(n * SUB, most).astype(bf16), NT, preferred_element_type=f32).astype(bf16)
    for start in range(0, rows, BLOCK):
        here = cluster_ref[:, start:start + BLOCK]
        rank = slot_ref[:, start:start + BLOCK] - here * most
        onehot = jnp.where(lax.broadcasted_iota(i32, (n * SUB, BLOCK), 0) // SUB == here, 1.0, 0.0).astype(bf16)
        found = jnp.dot(turned, onehot, preferred_element_type=f32)
        found = jnp.where(lax.broadcasted_iota(i32, (most, BLOCK), 0) == rank, found, 0.0)
        out_ref[:, start:start + BLOCK] = jnp.sum(found, axis=0, keepdims=True)

    @pl.loop(1, n)
    def _(slot):
        back_copy(slot, me).wait_send()


def per_device(embeddings, assignment, order_key):
    rows, width = embeddings.shape
    n_split = lax.axis_size("split")
    n = lax.axis_size("dp") * n_split
    most = 3 * rows // (2 * n)
    f32, bf16 = jnp.float32, jnp.bfloat16
    vmem = pl.BlockSpec(memory_space=pltpu.VMEM)
    dma = pltpu.SemaphoreType.DMA((n,))
    nearest = pl.pallas_call(
        functools.partial(kernel, n, n_split, most),
        out_shape=jax.ShapeDtypeStruct((1, rows), f32),
        in_specs=[pl.BlockSpec(memory_space=pl.ANY), vmem, vmem],
        out_specs=vmem,
        scratch_shapes=[
            pltpu.VMEM((rows, width), bf16),
            pltpu.SemaphoreType.DMA,
            pltpu.VMEM((1, rows), jnp.int32),
            pltpu.VMEM((n, most, width), bf16),
            pltpu.VMEM((n, 1, most), f32),
            pltpu.VMEM((n, most, width), bf16),
            pltpu.VMEM((n, 1, most), f32),
            pltpu.VMEM((n, SUB, most), f32),
            pltpu.VMEM((n, most, most), f32),
            pltpu.VMEM((n, SUB, most), f32),
            pltpu.VMEM((n, 1, most), f32),
            pltpu.VMEM((n, 1, most), f32),
            pltpu.VMEM((n, SUB, most), f32),
            dma, dma, dma, dma, dma, dma,
        ],
        compiler_params=pltpu.CompilerParams(collective_id=0, has_side_effects=True, vmem_limit_bytes=56 * 1024 * 1024),
    )(embeddings, assignment.reshape(1, rows), order_key.reshape(1, rows))
    return nearest.reshape(rows)


def solution(mesh):
    placed = (
        P(("groups", "dp", "split"), None),
        P(("groups", "dp", "split"), None),
        P(("groups", "dp", "split")),
    )
    return jax.shard_map(
        per_device,
        mesh=mesh,
        in_specs=placed,
        out_specs=P(("groups", "dp", "split")),
        check_vma=False,
    )
```

```python
import functools

import jax
import jax.numpy as jnp
from jax import lax
from jax.experimental import pallas as pl
from jax.experimental.pallas import tpu as pltpu
from jax.sharding import PartitionSpec as P

epsilon = 1e-06
MESH = pl.DeviceIdType.MESH
NT = (((1,), (1,)), ((), ()))
BLOCK = 256
SUB = 8
GROUP = 5


def xor(a, b, n):
    total, bit = 0, 1
    while bit < n:
        p, q = (a // bit) % 2, (b // bit) % 2
        total = total + (p + q - 2 * p * q) * bit
        bit *= 2
    return total


def offset_of(slot, n):
    t = slot - 1
    h = n // 2
    far = slot // (h + 2)
    first = (h + 2 - slot) // h
    return (1 - far) * (first * (h + t) + (1 - first) * (t - 1)) + far * (slot % n)


def kernel(n, n_split, most, rows_hbm, cluster_ref, key_ref, out_ref,
           rows_ref, rows_sem, slot_ref, send, send_key, recv, recv_key, lane_key, sub_key, best, back_send, back, back_parts,
           row_ssem, row_rsem, key_ssem, key_rsem, back_ssem, back_rsem):
    f32, bf16, i32 = jnp.float32, jnp.bfloat16, jnp.int32
    rows = rows_ref.shape[0]
    fetch = pltpu.make_async_copy(rows_hbm, rows_ref, rows_sem)
    fetch.start()
    me = lax.axis_index("dp") * n_split + lax.axis_index("split")

    def device(slot):
        partner = xor(me, offset_of(slot, n), n)
        return {"dp": partner // n_split, "split": partner % n_split}

    barrier = pltpu.get_barrier_semaphore()

    @pl.loop(1, n)
    def _(slot):
        pl.semaphore_signal(barrier, inc=1, device_id=device(slot), device_id_type=MESH)

    before = (lax.broadcasted_iota(i32, (BLOCK, BLOCK), 0) < lax.broadcasted_iota(i32, (BLOCK, BLOCK), 1))
    before = jnp.where(before, 1.0, 0.0).astype(bf16)
    carry = jnp.zeros((n, 1), f32)
    for start in range(0, rows, BLOCK):
        here = cluster_ref[:, start:start + BLOCK]
        onehot = jnp.where(lax.broadcasted_iota(i32, (n, BLOCK), 0) == here, 1.0, 0.0)
        earlier = jnp.dot(onehot.astype(bf16), before, preferred_element_type=f32) + carry
        carry = carry + jnp.sum(onehot, axis=1, keepdims=True)
        rank = jnp.sum(onehot * earlier, axis=0, keepdims=True).astype(i32)
        slot_ref[:, start:start + BLOCK] = here * most + rank

    key = key_ref[...]
    digit = lax.broadcasted_iota(i32, (SUB, rows), 0)
    digits = jnp.where(digit == 0, key // 16384, jnp.where(digit == 1, (key // 128) % 128, jnp.where(digit == 2, key % 128, jnp.where(digit == 3, 1, 0))))
    digits = digits.astype(f32).astype(bf16)

    place = lax.broadcasted_iota(i32, (SUB, SUB), 1)
    combine = jnp.where(place == 0, 16384.0, jnp.where(place == 1, 128.0, jnp.where(place == 2, 1.0, jnp.where(place == 3, -4194304.0, 0.0)))).astype(bf16)
    part = lax.broadcasted_iota(i32, (SUB, most), 0)

    def parts_of(row):
        whole = jnp.broadcast_to(row, (SUB, most))
        high = whole.astype(bf16).astype(f32)
        middle = (whole - high).astype(bf16).astype(f32)
        low = (whole - high) - middle
        return jnp.where(part == 0, high, jnp.where(part == 1, middle, jnp.where(part == 2, low, 0.0)))

    same = lax.broadcasted_iota(i32, (most, most), 0) == lax.broadcasted_iota(i32, (most, most), 1)
    identity = jnp.where(same, 1.0, 0.0).astype(bf16)

    def pack(cluster):
        place = slot_ref[...] - cluster * most
        pick = jnp.where(lax.broadcasted_iota(i32, (most, rows), 0) == place, 1.0, 0.0).astype(bf16)
        values = jnp.dot(pick, rows_ref[...], preferred_element_type=f32)
        scale = lax.rsqrt(jnp.sum(values * values, axis=1, keepdims=True) + epsilon)
        picked = lax.dot_general(digits, pick, NT, preferred_element_type=f32)
        return (values * scale).astype(bf16), jnp.dot(combine, picked.astype(bf16), preferred_element_type=f32)[:1]

    def row_copy(slot):
        return pltpu.make_async_remote_copy(send.at[slot], recv.at[slot], row_ssem.at[slot], row_rsem.at[slot], device_id=device(slot), device_id_type=MESH)

    def key_copy(slot):
        return pltpu.make_async_remote_copy(send_key.at[slot], recv_key.at[slot], key_ssem.at[slot], key_rsem.at[slot], device_id=device(slot), device_id_type=MESH)

    def back_copy(slot, cluster):
        return pltpu.make_async_remote_copy(back_send.at[slot], back.at[cluster], back_ssem.at[slot], back_rsem.at[slot], device_id=device(slot), device_id_type=MESH)

    fetch.wait()
    send[1], send_key[1] = pack(xor(me, offset_of(1, n), n))
    pl.semaphore_wait(barrier, n - 1)

    @pl.loop(2, n + 1)
    def _(slot):
        row_copy(slot - 1).start()
        key_copy(slot - 1).start()
        at = slot % n
        packed, packed_key = pack(xor(me, offset_of(slot, n), n))
        send[at] = packed
        send_key[at] = packed_key

    def take(slot, row):
        lane_key[slot] = jnp.broadcast_to(row, (SUB, most))
        turned = lax.dot_general(identity, parts_of(row).astype(bf16), NT, preferred_element_type=f32).astype(bf16)
        sub_key[slot] = jnp.dot(turned, jnp.ones((SUB, most), bf16), preferred_element_type=f32)

    def tile(columns, columns_key, own, own_key):
        sims = lax.dot_general(columns, own, NT, preferred_element_type=f32)
        seen = jnp.where(columns_key < own_key, sims, -1.0)
        return jnp.max(seen.reshape(most // SUB, SUB, most), axis=0)

    recv[0] = send[0]
    take(0, send_key[0])
    best[0] = jnp.maximum(tile(recv[0], sub_key[0], recv[0], lane_key[0][:1]), -1.0)

    @pl.loop(1, n)
    def _(u):
        row_copy(u).wait_recv()
        key_copy(u).wait_recv()
        new = recv[u]
        take(u, recv_key[u])
        new_lane, new_sub = lane_key[u][:1], sub_key[u]

        def meet(i, running):
            other = recv[i]
            best[i] = jnp.maximum(best[i], tile(new, new_sub, other, lane_key[i][:1]))
            return jnp.maximum(running, tile(other, sub_key[i], new, new_lane))

        def meet_group(group, running):
            for i in range(GROUP):
                running = meet(group * GROUP + i, running)
            return running

        running = lax.fori_loop(0, u // GROUP, meet_group, tile(new, new_sub, new, new_lane))
        best[u] = lax.fori_loop(u // GROUP * GROUP, u, meet, running)

    back_send[n - 1] = jnp.max(best[n - 1], axis=0, keepdims=True)

    @pl.loop(2, n)
    def _(step):
        back_send[n - step] = jnp.max(best[n - step], axis=0, keepdims=True)
        back_copy(n - step + 1, me).start()

    back_copy(1, me).start()
    back_parts[me] = parts_of(jnp.max(best[0], axis=0, keepdims=True))

    @pl.loop(1, n)
    def _(slot):
        row_copy(slot).wait_send()
        key_copy(slot).wait_send()

    @pl.loop(1, n)
    def _(slot):
        cluster = xor(me, offset_of(slot, n), n)
        back_copy(slot, cluster).wait_recv()
        back_parts[cluster] = parts_of(back[cluster])

    turned = lax.dot_general(identity, back_parts[...].reshape(n * SUB, most).astype(bf16), NT, preferred_element_type=f32).astype(bf16)
    for start in range(0, rows, BLOCK):
        here = cluster_ref[:, start:start + BLOCK]
        rank = slot_ref[:, start:start + BLOCK] - here * most
        onehot = jnp.where(lax.broadcasted_iota(i32, (n * SUB, BLOCK), 0) // SUB == here, 1.0, 0.0).astype(bf16)
        found = jnp.dot(turned, onehot, preferred_element_type=f32)
        found = jnp.where(lax.broadcasted_iota(i32, (most, BLOCK), 0) == rank, found, 0.0)
        out_ref[:, start:start + BLOCK] = jnp.sum(found, axis=0, keepdims=True)

    @pl.loop(1, n)
    def _(slot):
        back_copy(slot, me).wait_send()


def per_device(embeddings, assignment, order_key):
    rows, width = embeddings.shape
    n_split = lax.axis_size("split")
    n = lax.axis_size("dp") * n_split
    most = 3 * rows // (2 * n)
    f32, bf16 = jnp.float32, jnp.bfloat16
    vmem = pl.BlockSpec(memory_space=pltpu.VMEM)
    dma = pltpu.SemaphoreType.DMA((n,))
    nearest = pl.pallas_call(
        functools.partial(kernel, n, n_split, most),
        out_shape=jax.ShapeDtypeStruct((1, rows), f32),
        in_specs=[pl.BlockSpec(memory_space=pl.ANY), vmem, vmem],
        out_specs=vmem,
        scratch_shapes=[
            pltpu.VMEM((rows, width), bf16),
            pltpu.SemaphoreType.DMA,
            pltpu.VMEM((1, rows), jnp.int32),
            pltpu.VMEM((n, most, width), bf16),
            pltpu.VMEM((n, 1, most), f32),
            pltpu.VMEM((n, most, width), bf16),
            pltpu.VMEM((n, 1, most), f32),
            pltpu.VMEM((n, SUB, most), f32),
            pltpu.VMEM((n, most, most), f32),
            pltpu.VMEM((n, SUB, most), f32),
            pltpu.VMEM((n, 1, most), f32),
            pltpu.VMEM((n, 1, most), f32),
            pltpu.VMEM((n, SUB, most), f32),
            dma, dma, dma, dma, dma, dma,
        ],
        compiler_params=pltpu.CompilerParams(collective_id=0, has_side_effects=True, vmem_limit_bytes=56 * 1024 * 1024),
    )(embeddings, assignment.reshape(1, rows), order_key.reshape(1, rows))
    return nearest.reshape(rows)


def solution(mesh):
    placed = (
        P(("groups", "dp", "split"), None),
        P(("groups", "dp", "split"), None),
        P(("groups", "dp", "split")),
    )
    return jax.shard_map(
        per_device,
        mesh=mesh,
        in_specs=placed,
        out_specs=P(("groups", "dp", "split")),
        check_vma=False,
    )
```

```python
import functools

import jax
import jax.numpy as jnp
from jax import lax
from jax.experimental import pallas as pl
from jax.experimental.pallas import tpu as pltpu
from jax.sharding import PartitionSpec as P

epsilon = 1e-06
MESH = pl.DeviceIdType.MESH
NT = (((1,), (1,)), ((), ()))
BLOCK = 256
SUB = 8
GROUP = 5


def xor(a, b, n):
    total, bit = 0, 1
    while bit < n:
        p, q = (a // bit) % 2, (b // bit) % 2
        total = total + (p + q - 2 * p * q) * bit
        bit *= 2
    return total


def offset_of(slot, n):
    t = slot - 1
    h = n // 2
    far = slot // (h + 3)
    first = (h + 3 - slot) // h
    return (1 - far) * (first * (h + t) + (1 - first) * (t - 2)) + far * (slot % n)


def kernel(n, n_split, most, rows_hbm, cluster_ref, key_ref, out_ref,
           rows_ref, rows_sem, slot_ref, send, send_key, recv, recv_key, lane_key, sub_key, best, back_send, back, back_parts,
           row_ssem, row_rsem, key_ssem, key_rsem, back_ssem, back_rsem):
    f32, bf16, i32 = jnp.float32, jnp.bfloat16, jnp.int32
    rows = rows_ref.shape[0]
    fetch = pltpu.make_async_copy(rows_hbm, rows_ref, rows_sem)
    fetch.start()
    me = lax.axis_index("dp") * n_split + lax.axis_index("split")

    def device(slot):
        partner = xor(me, offset_of(slot, n), n)
        return {"dp": partner // n_split, "split": partner % n_split}

    barrier = pltpu.get_barrier_semaphore()

    @pl.loop(1, n)
    def _(slot):
        pl.semaphore_signal(barrier, inc=1, device_id=device(slot), device_id_type=MESH)

    before = (lax.broadcasted_iota(i32, (BLOCK, BLOCK), 0) < lax.broadcasted_iota(i32, (BLOCK, BLOCK), 1))
    before = jnp.where(before, 1.0, 0.0).astype(bf16)
    carry = jnp.zeros((n, 1), f32)
    for start in range(0, rows, BLOCK):
        here = cluster_ref[:, start:start + BLOCK]
        onehot = jnp.where(lax.broadcasted_iota(i32, (n, BLOCK), 0) == here, 1.0, 0.0)
        earlier = jnp.dot(onehot.astype(bf16), before, preferred_element_type=f32) + carry
        carry = carry + jnp.sum(onehot, axis=1, keepdims=True)
        rank = jnp.sum(onehot * earlier, axis=0, keepdims=True).astype(i32)
        slot_ref[:, start:start + BLOCK] = here * most + rank

    key = key_ref[...]
    digit = lax.broadcasted_iota(i32, (SUB, rows), 0)
    digits = jnp.where(digit == 0, key // 16384, jnp.where(digit == 1, (key // 128) % 128, jnp.where(digit == 2, key % 128, jnp.where(digit == 3, 1, 0))))
    digits = digits.astype(f32).astype(bf16)

    place = lax.broadcasted_iota(i32, (SUB, SUB), 1)
    combine = jnp.where(place == 0, 16384.0, jnp.where(place == 1, 128.0, jnp.where(place == 2, 1.0, jnp.where(place == 3, -4194304.0, 0.0)))).astype(bf16)
    part = lax.broadcasted_iota(i32, (SUB, most), 0)

    def parts_of(row):
        whole = jnp.broadcast_to(row, (SUB, most))
        high = whole.astype(bf16).astype(f32)
        middle = (whole - high).astype(bf16).astype(f32)
        low = (whole - high) - middle
        return jnp.where(part == 0, high, jnp.where(part == 1, middle, jnp.where(part == 2, low, 0.0)))

    same = lax.broadcasted_iota(i32, (most, most), 0) == lax.broadcasted_iota(i32, (most, most), 1)
    identity = jnp.where(same, 1.0, 0.0).astype(bf16)

    def pack(cluster):
        place = slot_ref[...] - cluster * most
        pick = jnp.where(lax.broadcasted_iota(i32, (most, rows), 0) == place, 1.0, 0.0).astype(bf16)
        values = jnp.dot(pick, rows_ref[...], preferred_element_type=f32)
        scale = lax.rsqrt(jnp.sum(values * values, axis=1, keepdims=True) + epsilon)
        picked = lax.dot_general(digits, pick, NT, preferred_element_type=f32)
        return (values * scale).astype(bf16), jnp.dot(combine, picked.astype(bf16), preferred_element_type=f32)[:1]

    def row_copy(slot):
        return pltpu.make_async_remote_copy(send.at[slot], recv.at[slot], row_ssem.at[slot], row_rsem.at[slot], device_id=device(slot), device_id_type=MESH)

    def key_copy(slot):
        return pltpu.make_async_remote_copy(send_key.at[slot], recv_key.at[slot], key_ssem.at[slot], key_rsem.at[slot], device_id=device(slot), device_id_type=MESH)

    def back_copy(slot, cluster):
        return pltpu.make_async_remote_copy(back_send.at[slot], back.at[cluster], back_ssem.at[slot], back_rsem.at[slot], device_id=device(slot), device_id_type=MESH)

    fetch.wait()
    send[1], send_key[1] = pack(xor(me, offset_of(1, n), n))
    pl.semaphore_wait(barrier, n - 1)

    @pl.loop(2, n + 1)
    def _(slot):
        row_copy(slot - 1).start()
        key_copy(slot - 1).start()
        at = slot % n
        packed, packed_key = pack(xor(me, offset_of(slot, n), n))
        send[at] = packed
        send_key[at] = packed_key

    def take(slot, row):
        lane_key[slot] = jnp.broadcast_to(row, (SUB, most))
        turned = lax.dot_general(identity, parts_of(row).astype(bf16), NT, preferred_element_type=f32).astype(bf16)
        sub_key[slot] = jnp.dot(turned, jnp.ones((SUB, most), bf16), preferred_element_type=f32)

    def tile(columns, columns_key, own, own_key):
        sims = lax.dot_general(columns, own, NT, preferred_element_type=f32)
        seen = jnp.where(columns_key < own_key, sims, -1.0)
        return jnp.max(seen.reshape(most // SUB, SUB, most), axis=0)

    recv[0] = send[0]
    take(0, send_key[0])
    best[0] = jnp.maximum(tile(recv[0], sub_key[0], recv[0], lane_key[0][:1]), -1.0)

    @pl.loop(1, n)
    def _(u):
        row_copy(u).wait_recv()
        key_copy(u).wait_recv()
        new = recv[u]
        take(u, recv_key[u])
        new_lane, new_sub = lane_key[u][:1], sub_key[u]

        def meet(i, running):
            other = recv[i]
            best[i] = jnp.maximum(best[i], tile(new, new_sub, other, lane_key[i][:1]))
            return jnp.maximum(running, tile(other, sub_key[i], new, new_lane))

        def meet_group(group, running):
            for i in range(GROUP):
                running = meet(group * GROUP + i, running)
            return running

        running = lax.fori_loop(0, u // GROUP, meet_group, tile(new, new_sub, new, new_lane))
        best[u] = lax.fori_loop(u // GROUP * GROUP, u, meet, running)

    back_send[n - 1] = jnp.max(best[n - 1], axis=0, keepdims=True)

    @pl.loop(2, n)
    def _(step):
        back_send[n - step] = jnp.max(best[n - step], axis=0, keepdims=True)
        back_copy(n - step + 1, me).start()

    back_copy(1, me).start()
    back_parts[me] = parts_of(jnp.max(best[0], axis=0, keepdims=True))

    @pl.loop(1, n)
    def _(slot):
        row_copy(slot).wait_send()
        key_copy(slot).wait_send()

    @pl.loop(1, n)
    def _(slot):
        cluster = xor(me, offset_of(slot, n), n)
        back_copy(slot, cluster).wait_recv()
        back_parts[cluster] = parts_of(back[cluster])

    turned = lax.dot_general(identity, back_parts[...].reshape(n * SUB, most).astype(bf16), NT, preferred_element_type=f32).astype(bf16)
    for start in range(0, rows, BLOCK):
        here = cluster_ref[:, start:start + BLOCK]
        rank = slot_ref[:, start:start + BLOCK] - here * most
        onehot = jnp.where(lax.broadcasted_iota(i32, (n * SUB, BLOCK), 0) // SUB == here, 1.0, 0.0).astype(bf16)
        found = jnp.dot(turned, onehot, preferred_element_type=f32)
        found = jnp.where(lax.broadcasted_iota(i32, (most, BLOCK), 0) == rank, found, 0.0)
        out_ref[:, start:start + BLOCK] = jnp.sum(found, axis=0, keepdims=True)

    @pl.loop(1, n)
    def _(slot):
        back_copy(slot, me).wait_send()


def per_device(embeddings, assignment, order_key):
    rows, width = embeddings.shape
    n_split = lax.axis_size("split")
    n = lax.axis_size("dp") * n_split
    most = 3 * rows // (2 * n)
    f32, bf16 = jnp.float32, jnp.bfloat16
    vmem = pl.BlockSpec(memory_space=pltpu.VMEM)
    dma = pltpu.SemaphoreType.DMA((n,))
    nearest = pl.pallas_call(
        functools.partial(kernel, n, n_split, most),
        out_shape=jax.ShapeDtypeStruct((1, rows), f32),
        in_specs=[pl.BlockSpec(memory_space=pl.ANY), vmem, vmem],
        out_specs=vmem,
        scratch_shapes=[
            pltpu.VMEM((rows, width), bf16),
            pltpu.SemaphoreType.DMA,
            pltpu.VMEM((1, rows), jnp.int32),
            pltpu.VMEM((n, most, width), bf16),
            pltpu.VMEM((n, 1, most), f32),
            pltpu.VMEM((n, most, width), bf16),
            pltpu.VMEM((n, 1, most), f32),
            pltpu.VMEM((n, SUB, most), f32),
            pltpu.VMEM((n, most, most), f32),
            pltpu.VMEM((n, SUB, most), f32),
            pltpu.VMEM((n, 1, most), f32),
            pltpu.VMEM((n, 1, most), f32),
            pltpu.VMEM((n, SUB, most), f32),
            dma, dma, dma, dma, dma, dma,
        ],
        compiler_params=pltpu.CompilerParams(collective_id=0, has_side_effects=True, vmem_limit_bytes=56 * 1024 * 1024),
    )(embeddings, assignment.reshape(1, rows), order_key.reshape(1, rows))
    return nearest.reshape(rows)


def solution(mesh):
    placed = (
        P(("groups", "dp", "split"), None),
        P(("groups", "dp", "split"), None),
        P(("groups", "dp", "split")),
    )
    return jax.shard_map(
        per_device,
        mesh=mesh,
        in_specs=placed,
        out_specs=P(("groups", "dp", "split")),
        check_vma=False,
    )
```
